32 devices in a mesh: grp: 1, frame: 32 (over z, y, x, core).
Axes of the slice: x: 2, y: 2, z: 4, core: 2. Of those that a mesh axis runs over, the one named last changes fastest.
Arguments:
- tokens: bfloat16 [8192, 2240], P(('grp', 'frame')), may hold values from -16 to 16
- w_query: bfloat16 [1792, 2240], P('frame'), may hold values from -0.125 to 0.125
- w_keyval: bfloat16 [3584, 2240], P('frame'), may hold values from -0.125 to 0.125
- taps: float32 [3, 1792], replicated, may hold values from -1 to 1
Outputs:
- mixed: bfloat16 [8192, 1792], P(('grp', 'frame'))
The draws below stay inside these ranges and needn't reach their ends.
All inputs are finite; a program needn't handle non-finite values.
Results may differ from the reference program's by a relative error of at most 0.0051.
Values may be sent and summed in bfloat16 or wider, within the bound.
A program may use at most 128 MiB of HBM per device.

```python
import jax
import jax.numpy as jnp
from jax import lax

D = 2240
HEADS = 16
HDIM = 112
HEIGHT = 32
WIDTH = 32
TOK_DEV = 256
FRAMES = 8
TOKENS = 8192
CH = 1792


def draw_tokens(key, part):
    key_noise, key_level, key_offset = jax.random.split(key, 3)
    blocks = TOKENS // TOK_DEV
    rising = 3.0 ** (jnp.arange(blocks, dtype=jnp.float32) / max(blocks - 1, 1))
    level = jax.random.uniform(key_level, (blocks, 1), jnp.float32, 0.7, 1.4) * rising[:, None]
    offsets = jax.random.normal(key_offset, (blocks, D), jnp.float32) * level
    noise = jax.random.normal(key_noise, (TOKENS, D), jnp.float32)
    values = noise + jnp.repeat(offsets, TOK_DEV, axis=0)
    return jnp.clip(values, -16.0, 16.0).astype(jnp.bfloat16)


def levels(rng, shape, cuts, smallest, high):
    gain = 1.0
    for axis_at, shards_of in cuts:
        heights = jax.random.uniform(jax.random.fold_in(jax.random.fold_in(rng, 6), axis_at), (shards_of,), jnp.float32, smallest / len(cuts), high / len(cuts))
        gain = gain * jnp.repeat(jnp.exp(heights), shape[axis_at] // shards_of).reshape((-1,) + (1,) * (len(shape) - 1 - axis_at))
    return gain


def scatter_about(own_key, dims, spread, bound, pieces=(), held_as=jnp.bfloat16):
    values = jax.random.normal(own_key, dims, jnp.float32) * spread
    if len(pieces) > 0:
        values = levels(own_key, dims, pieces, -0.22, 0.18) * values
    return jnp.clip(values, min=-bound, max=bound).astype(held_as)


def setup_inputs(seed: int = 0, part: int = 0) -> dict:
    keys = jax.random.split(jax.random.key(seed), 5)
    part_keys = jax.random.split(jax.random.fold_in(keys[4], part), 5)
    return {
        "tokens": draw_tokens(jax.random.fold_in(jax.random.fold_in(keys[4], part), 71), part),
        "w_query": scatter_about(keys[1], (CH, D), D ** -0.5, 0.125, ((0, 32),)),
        "w_keyval": scatter_about(keys[2], (2 * CH, D), D ** -0.5, 0.125, ((0, 32),)),
        "taps": jnp.clip(jax.random.uniform(keys[3], (3, CH), jnp.float32, -1.0, 1.0), -1.0, 1.0),
    }


epsilon = 1e-06

def normalize(rows_in):
    values = rows_in.astype(jnp.float32)
    scale_inv = lax.rsqrt(lax.optimization_barrier(jnp.mean(values * values, axis=-1, keepdims=True)) + epsilon)
    return (values * scale_inv).astype(jnp.bfloat16)

def temporal_mix(by_frame, taps):
    zeros_row = jnp.zeros_like(by_frame[:1])
    earlier = jnp.concatenate([zeros_row, by_frame[:-1]], 0)
    later_frame = jnp.concatenate([by_frame[1:], zeros_row], 0)
    return taps[0] * earlier + taps[1] * by_frame + taps[2] * later_frame

def reference(tokens, w_query, w_keyval, taps):
    channels = HEADS * HDIM
    blocks = TOKENS // TOK_DEV

    def project(block_rows):
        normed = normalize(block_rows)
        query_lin = jnp.dot(normed, w_query.T, preferred_element_type=jnp.float32)
        keyval_lin = jnp.dot(normed, w_keyval.T, preferred_element_type=jnp.float32)
        query_feats = jax.nn.relu(query_lin).astype(jnp.bfloat16)
        key_feats = jax.nn.relu(keyval_lin[:, :channels]).astype(jnp.bfloat16)
        value_proj = keyval_lin[:, channels:].astype(jnp.bfloat16)
        key_heads = key_feats.astype(jnp.float32).reshape(-1, HEADS, HDIM)
        value_heads = value_proj.astype(jnp.float32).reshape(-1, HEADS, HDIM)
        state = jnp.einsum('thd,the->hde', key_heads, value_heads, precision=lax.Precision.HIGHEST)
        return (query_feats, state, lax.optimization_barrier(jnp.sum(key_heads, axis=0)))
    query_feats, states, key_sums = lax.map(project, tokens.reshape(blocks, TOK_DEV, D))
    state = lax.optimization_barrier(jnp.sum(states, axis=0))
    key_total = lax.optimization_barrier(jnp.sum(key_sums, axis=0))
    query_heads = query_feats.reshape(TOKENS, HEADS, HDIM).astype(jnp.float32)
    numer = jnp.einsum('thd,hde->the', query_heads, state, precision=lax.Precision.HIGHEST)
    denom = jnp.einsum('thd,hd->th', query_heads, key_total, precision=lax.Precision.HIGHEST) + epsilon
    attended = (numer / denom[:, :, None]).reshape(TOKENS, channels).astype(jnp.bfloat16)
    by_frame = attended.reshape(FRAMES, HEIGHT * WIDTH, channels).astype(jnp.float32)
    return temporal_mix(by_frame, taps).reshape(TOKENS, channels).astype(jnp.bfloat16)
```

```python
import jax
import jax.numpy as jnp
from jax import lax
from jax.experimental import pallas as pl
from jax.experimental.pallas import tpu as pltpu
from jax.sharding import PartitionSpec as P

HEADS = 16
HDIM = 112
HEIGHT = 32
WIDTH = 32


epsilon = 1e-06


def from_behind(value, axis, steps):
    count = lax.axis_size(axis)
    leading, last = (max(0, -steps), min(count, count - steps))
    return lax.ppermute(value, axis, [(source, source + steps) for source in range(leading, last)])


def normalize(rows_in):
    values = rows_in.astype(jnp.float32)
    scale_inv = lax.rsqrt(jnp.mean(values * values, axis=-1, keepdims=True) + epsilon)
    return (values * scale_inv).astype(jnp.bfloat16)


def local(tokens, w_query, w_keyval, taps):
    channels = HEADS * HDIM
    rows_here = tokens.shape[0]
    normed = normalize(tokens)

    def project_rows(weight_rows):
        return lax.dot_general(
            normed, weight_rows, (((1,), (1,)), ((), ())), preferred_element_type=jnp.float32
        )

    keyval_lin = project_rows(lax.all_gather(w_keyval, "frame", axis=0, tiled=True))
    key_feats = jax.nn.relu(keyval_lin[:, :channels]).astype(jnp.bfloat16)
    value_proj = keyval_lin[:, channels:].astype(jnp.bfloat16)
    key_heads = key_feats.reshape(rows_here, HEADS, HDIM)
    value_heads = value_proj.reshape(rows_here, HEADS, HDIM)
    local_state = jnp.einsum(
        "thd,the->hde", key_heads, value_heads, preferred_element_type=jnp.float32
    )
    local_keys = jnp.sum(key_heads.astype(jnp.float32), axis=0)
    query_lin = project_rows(lax.all_gather(w_query, "frame", axis=0, tiled=True))
    query_feats = jax.nn.relu(query_lin).astype(jnp.bfloat16)
    state, key_total = lax.psum((local_state, local_keys), "frame")
    query_heads = query_feats.reshape(rows_here, HEADS, HDIM).astype(jnp.float32)
    numer = jnp.einsum("thd,hde->the", query_heads, state, precision=lax.Precision.HIGHEST)
    denom = (
        jnp.einsum("thd,hd->th", query_heads, key_total, precision=lax.Precision.HIGHEST) + epsilon
    )
    attended = (numer / denom[:, :, None]).reshape(rows_here, channels).astype(jnp.bfloat16)
    strips = HEIGHT * WIDTH // rows_here
    earlier = from_behind(attended, "frame", strips)
    later_frame = from_behind(attended, "frame", -strips)
    mixed = (
        taps[0] * earlier.astype(jnp.float32)
        + taps[1] * attended.astype(jnp.float32)
        + taps[2] * later_frame.astype(jnp.float32)
    ).astype(jnp.bfloat16)
    return mixed


COLUMNS = 4
CORES = 2
LAYER = COLUMNS * CORES
LOWEST = -3.0e38
NT = (((1,), (1,)), ((), ()))


def fused_kernel(depth, tok_ref, wq_ref, wkv_ref, taps_ref, out_ref,
                 tokbuf, scale, wqb, wkvb, queries, feats, st, sib_in, st_out, st_in, st_sum, full,
                 halo, mixbuf, tapbuf, tapcol,
                 local_sem, move_send, wrecv, zsend, sibsend, trecv, tsend, tfsend,
                 s1_send, s1_recv, s2_send, s2_recv, s3_send, s3_recv,
                 hsend, hrecv, osend, orecv):
    me = lax.axis_index("frame")
    z = me // LAYER
    inner = me % LAYER
    col = inner // CORES
    core = inner % CORES
    other = 1 - core
    yy = col // 2
    xx = col % 2

    def dev(layer, column, which):
        return {"frame": layer * LAYER + column * CORES + which}

    def near(o):
        return 2 * ((yy + o // 2) % 2) + (xx + o % 2) % 2

    def inside(layer):
        return jnp.logical_and(layer >= 0, layer < depth)

    sib = dev(z, col, other)

    def rcopy(src, dst, ssem, rsem, to):
        return pltpu.make_async_remote_copy(
            src_ref=src, dst_ref=dst, send_sem=ssem, recv_sem=rsem,
            device_id=to, device_id_type=pl.DeviceIdType.MESH)

    barrier = pltpu.get_barrier_semaphore()
    for step in range(1, LAYER):
        pl.semaphore_signal(barrier, inc=1, device_id={"frame": z * LAYER + (inner + step) % LAYER},
                            device_id_type=pl.DeviceIdType.MESH)
    for step in range(1, depth):
        for which in range(CORES):
            pl.semaphore_signal(barrier, inc=1, device_id=dev((z + step) % depth, col, which),
                                device_id_type=pl.DeviceIdType.MESH)

    to_col = inner % COLUMNS
    to_core = inner // COLUMNS
    keep = jnp.logical_and(to_col == col, to_core == core)

    def move():
        return rcopy(wkv_ref, wkvb.at[z, to_core], move_send.at[0], wrecv.at[z, 1, to_core], dev(z, to_col, to_core))

    kv_local = pltpu.make_async_copy(wkv_ref, wkvb.at[z, core], local_sem.at[1])
    q_local = pltpu.make_async_copy(wq_ref, wqb.at[z, core], local_sem.at[0])
    tok_local = pltpu.make_async_copy(tok_ref, tokbuf.at[col], local_sem.at[2])

    @pl.when(keep)
    def _():
        kv_local.start()

    pl.semaphore_wait(barrier, LAYER - 1 + (depth - 1) * CORES)

    @pl.when(jnp.logical_not(keep))
    def _():
        move().start()

    def wslot(t, part, c):
        return (wqb, wkvb)[part].at[t, c]

    def zcopy(t, part, way, src=None):
        slot = wslot(t, part, core)
        return rcopy(slot if src is None else src, slot, zsend.at[(way + 1) // 2, t, part],
                     wrecv.at[t, part, core], dev(z + way, col, core))

    def sibcopy(t, part, src=None):
        slot = wslot(t, part, core)
        return rcopy(slot if src is None else src, slot, sibsend.at[t, part], wrecv.at[t, part, core], sib)

    def send(t, part, way, src=None):
        @pl.when(inside(z + way))
        def _():
            zcopy(t, part, way, src).start()

    def arrive(k, part, way, onward):
        t = z - way * k

        @pl.when(inside(t))
        def _():
            sibcopy(t, part).wait_recv()
            if onward:
                send(t, part, way)
            sibcopy(t, part).start()

    def onward_query(way, early):
        far = inside(z - 2 * way)

        @pl.when(jnp.logical_and(inside(z - way), far if early else jnp.logical_not(far)))
        def _():
            send(z - way, 0, way)

    def sib_wait(k, part):
        for way in ((1, -1) if k else (1,)):
            t = z - way * k

            @pl.when(inside(t))
            def _():
                slot = wslot(t, part, other)
                rcopy(slot, slot, sibsend.at[t, part], wrecv.at[t, part, other], sib).wait_recv()

    side = (None, dev(z, near(1), core), dev(z, near(2), core))

    def tcopy(o, h):
        return rcopy(tok_ref.at[h], tokbuf.at[col, h], tsend.at[o - 1, h], trecv.at[col, h], side[o])

    def tforward(o):
        b, h = near(o), o - 1
        return rcopy(tokbuf.at[b, h], tokbuf.at[b, h], tfsend.at[o - 1], trecv.at[b, h], side[3 - o])

    def twait(o, h):
        b = near(o)
        rcopy(tokbuf.at[b, h], tokbuf.at[b, h], tfsend.at[0], trecv.at[b, h], side[1]).wait_recv()

    for way in (1, -1):
        send(z, 0, way, wq_ref)
    tcopy(1, 0).start()
    tcopy(2, 1).start()
    sibcopy(z, 0, wq_ref).start()
    tcopy(1, 1).start()
    tcopy(2, 0).start()
    q_local.start()
    tok_local.start()

    def norm(b, source):
        squares = 0.0
        for h in range(2):
            values = source(h).astype(jnp.float32)
            squares = squares + jnp.sum(values * values, axis=0, keepdims=True)
        scale[b] = lax.rsqrt(squares / (2 * tok_ref.shape[1]) + epsilon)

    norm(col, lambda h: tok_ref[h])

    @pl.when(keep)
    def _():
        kv_local.wait()

    @pl.when(jnp.logical_not(keep))
    def _():
        rcopy(wkv_ref, wkvb.at[z, core], move_send.at[0], wrecv.at[z, 1, core], sib).wait_recv()

    for way in (1, -1):
        send(z, 1, way)
    sibcopy(z, 1).start()
    q_local.wait()
    tok_local.wait()

    def tokens_of(b):
        return tokbuf[b].reshape(tokbuf.shape[1] * tokbuf.shape[2], tokbuf.shape[3])

    def project_query(t, o):
        b = near(o)
        toks = tokens_of(b)
        parts = [jnp.dot(wqb[t, c], toks, preferred_element_type=jnp.float32) for c in range(2)]
        query = jnp.concatenate(parts, axis=0) * scale[b]
        queries[t, b] = jnp.maximum(query, 0.0).astype(jnp.bfloat16)

    def project_keyval(t, o):
        b = near(o)
        kv = wkvb[t].reshape(2 * wkvb.shape[2], wkvb.shape[3])
        lin = jnp.dot(kv, tokens_of(b), preferred_element_type=jnp.float32) * scale[b]
        floor = jnp.where(t < depth // 2, 0.0, LOWEST)
        lin = jnp.maximum(lin, floor).astype(jnp.bfloat16)
        feats[t, b, 0] = lin[:HDIM]
        feats[t, b, 1] = lin[HDIM:]

    def compute(works, count, offset_of, o_from, o_count):
        def body(i, carry):
            t = z + offset_of(i // o_count)

            @pl.when(inside(t))
            def _():
                for work in works:
                    work(t, o_from + i % o_count)
            return carry
        lax.fori_loop(0, count * o_count, body, 0)

    def norm_recv(o):
        b = near(o)
        norm(b, lambda h: tokbuf[b, h])

    for way in (1, -1):
        arrive(1, 0, way, False)
        onward_query(way, True)

    own = (lax.broadcasted_iota(jnp.int32, (tapbuf.shape[0], HDIM), 0))
    picked = jnp.zeros((tapbuf.shape[0], HDIM), jnp.float32)
    for t in range(depth):
        for c in range(COLUMNS):
            at = (t * COLUMNS + c) * HDIM
            rows_here = taps_ref[:, at:at + HDIM]
            for k in range(3):
                mine_now = jnp.logical_and(own == k * depth + t, col == c)
                picked = jnp.where(mine_now, rows_here[k:k + 1], picked)
    tapbuf[...] = jnp.zeros(tapbuf.shape, tapbuf.dtype)
    tapbuf[:, :HDIM] = picked
    turned = tapbuf[...].T
    for t in range(depth):
        for k in range(3):
            at = k * depth + t
            tapcol[t, k] = jnp.broadcast_to(turned[:HDIM, at:at + 1], (HDIM, tapcol.shape[3]))

    sib_wait(0, 0)
    sib_wait(0, 1)
    compute((project_query, project_keyval), 1, lambda i: 0, 0, 1)
    sib_wait(1, 0)
    compute((project_query,), 2, lambda i: 2 * i - 1, 0, 1)
    twait(1, 0)
    tforward(1).start()
    twait(2, 1)
    tforward(2).start()
    for way in (1, -1):
        arrive(1, 1, way, True)
        onward_query(way, False)
    sib_wait(1, 1)
    compute((project_keyval,), 2, lambda i: 2 * i - 1, 0, 1)
    for way in (1, -1):
        arrive(2, 1, way, True)
    twait(1, 1)
    norm_recv(1)
    twait(2, 0)
    norm_recv(2)
    compute((project_query, project_keyval), 3, lambda i: i - 1, 1, 2)
    sib_wait(2, 1)
    compute((project_keyval,), 2, lambda i: 4 * i - 2, 0, 3)
    for way in (1, -1):
        arrive(2, 0, way, True)
    sib_wait(2, 0)
    compute((project_query,), 2, lambda i: 4 * i - 2, 0, 3)
    twait(3, 0)
    twait(3, 1)
    norm_recv(3)
    compute((project_keyval,), 5, lambda i: i - 2, 3, 1)
    for way in (1, -1):
        arrive(3, 1, way, False)
    sib_wait(3, 1)
    compute((project_keyval,), 2, lambda i: 6 * i - 3, 0, 4)

    half = depth // 2
    ones = jnp.ones((st.shape[1] - HDIM, feats.shape[4]), jnp.bfloat16)
    for t in range(depth):
        total = None
        for b in range(COLUMNS):
            values = jnp.concatenate([feats[half + t // 2, b, t % 2], ones], axis=0)
            term = lax.dot_general(values, feats[t // 2, b, t % 2], NT, preferred_element_type=jnp.float32)
            total = term if total is None else total + term
        st[t] = total
    first = rcopy(st.at[pl.ds(2 * other, 2)], sib_in, s1_send.at[0], s1_recv.at[0], sib)
    first.start()
    first.wait()
    mine = (st[pl.ds(2 * core, 2)] + sib_in[...]).astype(jnp.bfloat16)
    st_out[...] = mine
    st_in[z] = mine

    def across(step):
        return rcopy(st_out, st_in.at[z], s2_send.at[step], s2_recv.at[z], dev((z + step) % depth, col, core))

    for step in range(1, depth):
        across(step).start()

    def hcopy(way, t):
        d = (way + 1) // 2
        return rcopy(queries.at[t, pl.ds(2 * d, 2)], halo.at[d, t], hsend.at[d, t], hrecv.at[d, t], dev(z + way, col, core))

    def order(layer, i):
        return jnp.where(layer < half, i, depth - 1 - i)

    for way in (1, -1):
        @pl.when(jnp.logical_not(inside(z - way)))
        def _():
            halo[(way + 1) // 2] = jnp.zeros(halo.shape[1:], halo.dtype)

    compute((project_query,), 5, lambda i: i - 2, 3, 1)

    def halo_send(way, i):
        t = order(z + way, i)

        @pl.when(inside(z + way))
        def _():
            hcopy(way, t).start()

    for i in range(depth - 1):
        for way in (1, -1):
            halo_send(way, i)

    for step in range(1, depth):
        came = (z + step) % depth
        rcopy(st_out, st_in.at[came], s2_send.at[step], s2_recv.at[came], sib).wait_recv()
    total = st_in[0].astype(jnp.float32)
    for t in range(1, depth):
        total = total + st_in[t].astype(jnp.float32)
    st_sum[...] = total
    full[pl.ds(2 * core, 2)] = total
    third = rcopy(st_sum, full.at[pl.ds(2 * core, 2)], s3_send.at[0], s3_recv.at[0], sib)
    third.start()
    rcopy(st_sum, full.at[pl.ds(2 * other, 2)], s3_send.at[0], s3_recv.at[0], sib).wait_recv()

    def ocopy(t, o):
        b = near(o)
        return rcopy(mixbuf.at[t, b], out_ref.at[t, col], osend.at[t, o], orecv.at[t, col], dev(z, b, core))

    def finish(i):
        t = order(z, i)
        for way in (1, -1):
            @pl.when(inside(z - way))
            def _():
                hcopy(way, t).wait_recv()
        whole = full[t]
        high = whole.astype(jnp.bfloat16)
        low = (whole - high.astype(jnp.float32)).astype(jnp.bfloat16)

        def attend(query):
            both = (jnp.dot(high, query, preferred_element_type=jnp.float32)
                    + jnp.dot(low, query, preferred_element_type=jnp.float32))
            return (both[:HDIM] / (both[HDIM:HDIM + 1] + epsilon)).astype(jnp.bfloat16).astype(jnp.float32)

        w = [jnp.concatenate([tapcol[t, k]] * (mixbuf.shape[3] // tapcol.shape[3]), axis=1) for k in range(3)]
        for x in range(2):
            even = attend(queries[t, x])
            odd = attend(queries[t, 2 + x])
            before = attend(halo[1, t, x])
            after = attend(halo[0, t, x])
            mixbuf[t, x] = (w[0] * before + w[1] * even + w[2] * odd).astype(jnp.bfloat16)
            mixbuf[t, 2 + x] = (w[0] * even + w[1] * odd + w[2] * after).astype(jnp.bfloat16)
        for o in (3, 1, 2):
            ocopy(t, o).start()
        out_ref[t, col] = mixbuf[t, col]

    def finish_step(i, carry):
        finish(i)
        return carry

    lax.fori_loop(0, depth - 1, finish_step, 0)
    for way in (1, -1):
        arrive(3, 0, way, False)
    sib_wait(3, 0)
    compute((project_query,), 2, lambda i: 6 * i - 3, 0, 4)
    for way in (1, -1):
        halo_send(way, depth - 1)
    finish(depth - 1)

    for t in range(depth):
        for o in range(1, COLUMNS):
            b = near(o)
            rcopy(mixbuf.at[t, b], out_ref.at[t, b], osend.at[t, o], orecv.at[t, b], dev(z, b, core)).wait_recv()
            ocopy(t, o).wait_send()
        for way in (1, -1):
            @pl.when(inside(z + way))
            def _():
                hcopy(way, t).wait_send()
    third.wait_send()
    for step in range(1, depth):
        across(step).wait_send()

    @pl.when(jnp.logical_not(keep))
    def _():
        move().wait_send()

    for o in (1, 2):
        for h in range(2):
            tcopy(o, h).wait_send()
        tforward(o).wait_send()
    for t in range(depth):
        for part in range(2):
            sibcopy(t, part).wait_send()
            for way in (1, -1):
                @pl.when(jnp.logical_and(way * (z - t) >= 0, inside(z + way)))
                def _():
                    zcopy(t, part, way).wait_send()


def fused(tokens, w_query, w_keyval, taps):
    rows, width = tokens.shape
    depth = lax.axis_size("frame") // LAYER
    bf16, f32 = jnp.bfloat16, jnp.float32
    dma = lambda *s: pltpu.SemaphoreType.DMA(s)
    ext = HDIM + 16
    vmem = pl.BlockSpec(memory_space=pltpu.VMEM)
    out = pl.pallas_call(
        lambda *refs: fused_kernel(depth, *refs),
        out_shape=jax.ShapeDtypeStruct((depth, COLUMNS, HDIM, rows), bf16),
        in_specs=[vmem] * 4,
        out_specs=vmem,
        scratch_shapes=[
            pltpu.VMEM((COLUMNS, 2, width // 2, rows), bf16),
            pltpu.VMEM((COLUMNS, 1, rows), f32),
            pltpu.VMEM((depth, 2, w_query.shape[0], width), bf16),
            pltpu.VMEM((depth, 2, w_keyval.shape[0], width), bf16),
            pltpu.VMEM((depth, COLUMNS, HDIM, rows), bf16),
            pltpu.VMEM((depth, COLUMNS, 2, HDIM, rows), bf16),
            pltpu.VMEM((depth, ext, HDIM), f32),
            pltpu.VMEM((2, ext, HDIM), f32),
            pltpu.VMEM((2, ext, HDIM), bf16),
            pltpu.VMEM((depth, 2, ext, HDIM), bf16),
            pltpu.VMEM((2, ext, HDIM), f32),
            pltpu.VMEM((depth, ext, HDIM), f32),
            pltpu.VMEM((2, depth, 2, HDIM, rows), bf16),
            pltpu.VMEM((depth, COLUMNS, HDIM, rows), bf16),
            pltpu.VMEM((128, 128), f32),
            pltpu.VMEM((depth, 3, HDIM, 128), f32),
            dma(3), dma(1), dma(depth, 2, 2), dma(2, depth, 2), dma(depth, 2),
            dma(COLUMNS, 2), dma(2, 2), dma(2),
            dma(1), dma(1), dma(depth), dma(depth), dma(1), dma(1),
            dma(2, depth), dma(2, depth), dma(depth, COLUMNS), dma(depth, COLUMNS),
        ],
        compiler_params=pltpu.CompilerParams(collective_id=0, has_side_effects=True, vmem_limit_bytes=60000 * 1024),
    )(tokens.T.reshape(2, width // 2, rows), w_query, w_keyval, taps)
    return out.reshape(HEADS * HDIM, rows).T


def fits(count, tokens, w_query, w_keyval):
    return (
        w_keyval.shape[0] // count == HDIM
        and 2 * w_query.shape[0] // count == HDIM
        and count % LAYER == 0
        and count // LAYER * COLUMNS == HEADS
        and HEIGHT * WIDTH // (tokens.shape[0] // count) == COLUMNS
    )


def solution(mesh):
    placed = (P(("grp", "frame"), None), P("frame", None), P("frame", None), P())

    def step(tokens, w_query, w_keyval, taps):
        groups, count = mesh.shape["grp"], mesh.shape["frame"]
        part = jax.ShapeDtypeStruct((tokens.shape[0] // groups,) + tokens.shape[1:], tokens.dtype)
        body = fused if fits(count, part, w_query, w_keyval) else local
        return jax.shard_map(
            body, mesh=mesh, in_specs=placed, out_specs=P(("grp", "frame"), None), check_vma=False
        )(tokens, w_query, w_keyval, taps)

    return step
```
